32 devices in a mesh: sec: 4 (over y, x), gx: 4 (over z), gy: 2 (over core).
Axes of the slice: x: 2, y: 2, z: 4, core: 2. Of those that a mesh axis runs over, the one named last changes fastest.
Arguments:
- driving: float32 [3, 128, 256], P(None, 'gx', 'gy'), may hold values from -6 to 6
- rate_factor: float32 [3, 128, 256], P(None, 'gx', 'gy'), may hold values from 0.5 to 4
- friction_init: float32 [3, 128, 256], P(None, 'gx', 'gy'), may hold values from 0.2 to 2
- ice_mask: int32 [3, 128, 256], P(None, 'gx', 'gy'), may hold values 0 or 1
- grounded_mask: int32 [3, 128, 256], P(None, 'gx', 'gy'), may hold values 0 or 1
- melt: float32 [3, 128, 256], P(None, 'gx', 'gy'), may hold values from 0.1 to 1
- transmissivity: float32 [3, 128, 256], P(None, 'gx', 'gy'), may hold values from 0.5 to 5
- leakage: float32 [3, 128, 256], P(None, 'gx', 'gy'), may hold values from 0.05 to 0.5
- overburden: float32 [3, 128, 256], P(None, 'gx', 'gy'), may hold values from 0.5 to 2
- friction_scale: float32 [3, 128, 256], P(None, 'gx', 'gy'), may hold values from 0.5 to 4
Outputs:
- column_out: float32 [4, 3, 128, 256], P('sec', None, 'gx', 'gy')
The draws below stay inside these ranges and needn't reach their ends.
All inputs are finite; a program needn't handle non-finite values. No bound on the sum of `ice_mask` or of `grounded_mask` on one device may be relied on, other than what follows from the above.
Results may differ from the reference program's by a relative error of at most 0.00002.
Values sent between devices are 32-bit elements; how exact they have to be, the bound alone decides.
A program may use at most 64 MiB of HBM per device.

```python
import math
import jax
import jax.numpy as jnp
from jax import lax

LAYERS = 40
PICARD = 2
SWEEPS = 4
STRIPS = 3
NX = 128
NY = 256


def plant(entries, key, least, high):
    longest = entries.shape.index(max(entries.shape))
    spots = []
    for shift in (0, 1):
        where = [jax.random.randint(jax.random.fold_in(key, axis), (), 0, length) for axis, length in enumerate(entries.shape)]
        where[longest] = (where[longest] + shift) % entries.shape[longest]
        spots.append(tuple(where))
    return entries.at[spots[0]].set(least).at[spots[1]].set(high)


def shard_levels(rng, dims, shards, least, largest):
    loudness = 1.0
    for dim, shards_of in shards:
        steps = jax.random.uniform(jax.random.fold_in(jax.random.fold_in(rng, 6), dim), (shards_of,), jnp.float32, least / len(shards), largest / len(shards))
        loudness = loudness * jnp.repeat(jnp.exp(steps), dims[dim] // shards_of).reshape((-1,) + (1,) * (len(dims) - 1 - dim))
    return loudness


def noise(stream_key, dims, width, reach, pieces=(), kind=jnp.bfloat16):
    values = jax.random.normal(stream_key, dims, jnp.float32) * width
    if len(pieces) > 0:
        values = shard_levels(stream_key, dims, pieces, -0.22, 0.18) * values
    return jnp.clip(values, min=-reach, max=reach).astype(kind)


def setup_inputs(seed: int = 0) -> dict:
    arg_keys = jax.random.split(jax.random.key(seed), 11)
    return {
        "driving": noise(arg_keys[0], (STRIPS, NX, NY), 1.0, 6.0, ((1, 4), (2, 2)), jnp.float32),
        "rate_factor": jnp.clip(jnp.exp(math.log(4.0) - 2.0794415 * jax.random.uniform(arg_keys[1], (STRIPS, NX, NY), jnp.float32) ** shard_levels(arg_keys[1], (STRIPS, NX, NY), ((1, 4), (2, 2)), -0.2, 0.2)), 0.5, 4.0),
        "friction_init": jnp.clip(jnp.exp(math.log(2.0) - 2.3025851 * jax.random.uniform(arg_keys[2], (STRIPS, NX, NY), jnp.float32) ** shard_levels(arg_keys[2], (STRIPS, NX, NY), ((1, 4), (2, 2)), -0.2, 0.2)), 0.2, 2.0),
        "ice_mask": plant((jax.random.randint(arg_keys[3], (STRIPS, NX, NY), 0, 10) < 9).astype(jnp.int32), jax.random.fold_in(arg_keys[3], 1), 0, 1),
        "grounded_mask": plant((jax.random.randint(arg_keys[4], (STRIPS, NX, NY), 0, 4) < 3).astype(jnp.int32), jax.random.fold_in(arg_keys[4], 1), 0, 1),
        "melt": jnp.clip(jnp.exp(math.log(1.0) - 2.3025851 * jax.random.uniform(arg_keys[5], (STRIPS, NX, NY), jnp.float32) ** shard_levels(arg_keys[5], (STRIPS, NX, NY), ((1, 4), (2, 2)), -0.2, 0.2)), 0.1, 1.0),
        "transmissivity": jnp.clip(jnp.exp(math.log(5.0) - 2.3025851 * jax.random.uniform(arg_keys[6], (STRIPS, NX, NY), jnp.float32) ** shard_levels(arg_keys[6], (STRIPS, NX, NY), ((1, 4), (2, 2)), -0.2, 0.2)), 0.5, 5.0),
        "leakage": jnp.clip(jnp.exp(math.log(0.5) - 2.3025851 * jax.random.uniform(arg_keys[7], (STRIPS, NX, NY), jnp.float32) ** shard_levels(arg_keys[7], (STRIPS, NX, NY), ((1, 4), (2, 2)), -0.2, 0.2)), 0.05, 0.5),
        "overburden": jnp.clip(jnp.exp(math.log(2.0) - 1.3862944 * jax.random.uniform(arg_keys[8], (STRIPS, NX, NY), jnp.float32) ** shard_levels(arg_keys[8], (STRIPS, NX, NY), ((1, 4), (2, 2)), -0.2, 0.2)), 0.5, 2.0),
        "friction_scale": jnp.clip(jnp.exp(math.log(4.0) - 2.0794415 * jax.random.uniform(arg_keys[9], (STRIPS, NX, NY), jnp.float32) ** shard_levels(arg_keys[9], (STRIPS, NX, NY), ((1, 4), (2, 2)), -0.2, 0.2)), 0.5, 4.0),
    }


VERT = 4.0
FLOOR = 0.25
HEATING = 0.5


def shifted(values_in):
    padded = jnp.pad(values_in, ((0, 0), (1, 1), (1, 1)))
    return padded[:, 2:, 1:-1], padded[:, :-2, 1:-1], padded[:, 1:-1, 2:], padded[:, 1:-1, :-2]


def ice_core(velocity, x_plus, x_minus, y_plus, y_minus, driving, rate_here, friction, icemask):
    layers = velocity.shape[0]
    vertical = jnp.concatenate([velocity[1:] - velocity[:-1], jnp.zeros_like(velocity[:1])], axis=0)
    strain = vertical * vertical + 0.25 * (x_plus - x_minus) ** 2 + 0.25 * (y_plus - y_minus) ** 2 + FLOOR
    viscous = rate_here * strain ** (-1.0 / 3.0)
    coupling = VERT * 0.5 * (viscous[:-1] + viscous[1:])
    right_side = driving + viscous * (x_plus + x_minus + y_plus + y_minus)
    ratios = []
    values = []
    for level_k in range(layers):
        pivot_k = 4.0 * viscous[level_k]
        term_k = right_side[level_k]
        if level_k < layers - 1:
            pivot_k = pivot_k + coupling[level_k]
        if level_k > 0:
            pivot_k = pivot_k + coupling[level_k - 1] - coupling[level_k - 1] * ratios[level_k - 1]
            term_k = term_k + coupling[level_k - 1] * values[level_k - 1]
        else:
            pivot_k = pivot_k + friction
        values.append(term_k / pivot_k)
        if level_k < layers - 1:
            ratios.append(coupling[level_k] / pivot_k)
    result = [values[-1]]
    for level_k in range(layers - 2, -1, -1):
        result.insert(0, values[level_k] + ratios[level_k] * result[0])
    return jnp.stack(result) * icemask


def water_sweep(pressure, trans_eff, leakage, source):
    press_views = shifted(pressure)
    trans_views = shifted(trans_eff)
    numerator = source
    denominator = leakage
    for trans_next, press_next in zip(trans_views, press_views):
        face_weight = 0.5 * (trans_eff + trans_next)
        numerator = numerator + face_weight * press_next
        denominator = denominator + face_weight
    return numerator / denominator


def reference(driving, rate_factor, friction_init, ice_mask, grounded_mask, melt, transmissivity, leakage, overburden, friction_scale):
    icemask = ice_mask.astype(jnp.float32)
    grounded = grounded_mask.astype(jnp.float32)
    friction = friction_init * grounded
    pressure = overburden
    velocity = jnp.zeros((STRIPS, LAYERS, NX, NY), jnp.float32)

    def solve_sector(parts):
        current, drive_in, rate_in, fric_in, mask_in = parts
        x_plus, x_minus, y_plus, y_minus = shifted(current)
        return ice_core(current, x_plus, x_minus, y_plus, y_minus, drive_in, rate_in, fric_in, mask_in)

    for picard in range(PICARD):
        velocity = lax.map(solve_sector, (velocity, driving, rate_factor, friction, icemask))
        sliding = velocity[:, 0]
        squared = sliding * sliding
        trans_eff = transmissivity * (1.0 + squared / (1.0 + squared))
        source = melt + HEATING * friction * squared
        for sweep_i in range(SWEEPS):
            pressure = water_sweep(pressure, trans_eff, leakage, source)
        friction = friction_scale * pressure * grounded
    ice_part = jnp.stack([velocity[:, -1], velocity[:, 0], friction], axis=1)
    return jnp.concatenate([ice_part, pressure[None]], axis=0)
```

```python
import functools

import jax
import jax.numpy as jnp
import numpy as np
from jax import lax
from jax.experimental import pallas as pl
from jax.experimental.pallas import tpu as pltpu
from jax.sharding import PartitionSpec as P

LAYERS = 40
SWEEPS = 4
VERT = 4.0
FLOOR = 0.25
HEATING = 0.5

RIM = 8
HALF = RIM // 2
RESCALE = 10
THIRD = -1.0 / (3.0 * float(np.log(2.0)))
DIRECTIONS = [(dx, dy) for dx in (-1, 0, 1) for dy in (-1, 0, 1) if (dx, dy) != (0, 0)]
MESH = pl.DeviceIdType.MESH


def basal_response():
    matrix = np.zeros((LAYERS, LAYERS))
    for k in range(LAYERS):
        matrix[k, k] = 4.0 + (VERT if k > 0 else 0.0) + (VERT if k < LAYERS - 1 else 0.0)
        if k > 0:
            matrix[k, k - 1] = matrix[k - 1, k] = -VERT
    unit = np.zeros(LAYERS)
    unit[0] = 1.0
    return np.linalg.solve(matrix, unit)


def turn(values, shift, axis):
    return pltpu.roll(values, shift % values.shape[axis], axis)


def neighbours(f):
    return turn(f, -1, 0), turn(f, 1, 0), turn(f, -1, 1), turn(f, 1, 1)


def water_solve(pressure, trans_eff, leakage, source, valid):
    faces = [0.5 * (trans_eff + t) for t in neighbours(trans_eff)]
    total = leakage + ((faces[0] + faces[1]) + (faces[2] + faces[3]))
    inverse = jnp.where(valid, 1.0 / total, 0.0)
    weights = [f * inverse for f in faces]
    base = source * inverse
    for _ in range(SWEEPS):
        parts = [w * p for w, p in zip(weights, neighbours(pressure))]
        pressure = base + ((parts[0] + parts[1]) + (parts[2] + parts[3]))
    return pressure


def kernel(sectors, nx, ny, *refs):
    ins = refs[:10]
    out = refs[10]
    floats, ints, pack_l, pack_r, rim_l, rim_r, q_ref, g_ref, r_ref, send_p = refs[11:21]
    in_sem, send_sem, recv_sem, last_send, last_recv = refs[21:]
    rows, lanes = ins[0].shape[1:]
    sec = lax.axis_index("sec")
    gx = lax.axis_index("gx")
    gy = lax.axis_index("gy")
    strip = lax.rem(sec, sectors)
    is_ice = sec < sectors
    sends_last = jnp.logical_and(sec > 0, is_ice)

    def exists(dx, dy):
        x, y = gx + dx, gy + dy
        return jnp.logical_and(
            jnp.logical_and(x >= 0, x < nx), jnp.logical_and(y >= 0, y < ny)
        )

    float_ids = (0, 1, 2, 5, 6, 7, 8, 9)
    int_ids = (3, 4)
    loads = []
    for slot, arg in enumerate(float_ids):
        loads.append(pltpu.make_async_copy(ins[arg].at[strip], floats.at[slot, pl.ds(RIM, rows)], in_sem.at[slot]))
    for slot, arg in enumerate(int_ids):
        loads.append(pltpu.make_async_copy(ins[arg].at[strip], ints.at[slot, pl.ds(RIM, rows)], in_sem.at[8 + slot]))
    for load in loads:
        load.start()

    barrier = pltpu.get_barrier_semaphore()
    count = jnp.int32(0)
    for dx, dy in DIRECTIONS:
        here = exists(dx, dy)
        count = count + here.astype(jnp.int32)

        @pl.when(here)
        def _(dx=dx, dy=dy):
            pl.semaphore_signal(barrier, inc=1, device_id={"gx": gx + dx, "gy": gy + dy}, device_id_type=MESH)

    count = count + sends_last.astype(jnp.int32)
    count = count + jnp.where(is_ice, 0, sectors - 1)

    @pl.when(sends_last)
    def _():
        pl.semaphore_signal(barrier, inc=1, device_id={"sec": sectors}, device_id_type=MESH)

    for s in range(1, sectors):

        @pl.when(jnp.logical_not(is_ice))
        def _(s=s):
            pl.semaphore_signal(barrier, inc=1, device_id={"sec": s}, device_id_type=MESH)

    for load in loads:
        load.wait()

    lane = lax.broadcasted_iota(jnp.int32, (rows, lanes), 1)
    fields = [floats[i, RIM : RIM + rows] for i in range(8)]
    fields += [ints[i, RIM : RIM + rows].astype(jnp.float32) for i in range(2)]
    left = jnp.zeros((rows, lanes), jnp.float32)
    right = jnp.zeros((rows, lanes), jnp.float32)
    for i, f in enumerate(fields):
        moved = turn(f, RIM * i, 1)
        group = lane // RIM
        left = jnp.where(group == i, moved, left)
        right = jnp.where(group == (i - 1) % (lanes // RIM), moved, right)
    pack_l[...] = left
    pack_r[...] = right

    pl.semaphore_wait(barrier, count)

    def copies(dx, dy, n):
        target = {"gx": gx + dx, "gy": gy + dy}

        def remote(src, dst, m):
            return pltpu.make_async_remote_copy(
                src_ref=src, dst_ref=dst, send_sem=send_sem.at[m], recv_sem=recv_sem.at[m],
                device_id=target, device_id_type=MESH,
            )

        if dy == 0:
            first = rows if dx > 0 else RIM
            landing = 0 if dx > 0 else RIM + rows
            return [
                remote(floats.at[:, pl.ds(first, RIM)], floats.at[:, pl.ds(landing, RIM)], n),
                remote(ints.at[:, pl.ds(first, RIM)], ints.at[:, pl.ds(landing, RIM)], n + 8),
            ]
        src, dst = (pack_r, rim_l) if dy > 0 else (pack_l, rim_r)
        if dx == 0:
            return [remote(src, dst.at[pl.ds(RIM, rows)], n)]
        first = rows - RIM if dx > 0 else 0
        landing = 0 if dx > 0 else RIM + rows
        return [remote(src.at[pl.ds(first, RIM)], dst.at[pl.ds(landing, RIM)], n)]

    order = sorted(range(8), key=lambda n: abs(DIRECTIONS[n][1]))
    for n in order:
        dx, dy = DIRECTIONS[n]

        @pl.when(exists(dx, dy))
        def _(dx=dx, dy=dy, n=n):
            for c in copies(dx, dy, n):
                c.start()

    for n in order:
        dx, dy = DIRECTIONS[n]

        @pl.when(exists(-dx, -dy))
        def _(dx=dx, dy=dy, n=n):
            for c in copies(dx, dy, n):
                c.wait_recv()

    ext = rows + 2 * RIM
    group = lax.broadcasted_iota(jnp.int32, (ext, lanes), 1) // RIM
    packed_l = rim_l[...]
    packed_r = rim_r[...]

    def extend(i, main):
        rim = turn(jnp.where(group == i, packed_r, packed_l), -RIM * i, 1)
        return jnp.concatenate([main, rim], axis=1)

    row_i = lax.broadcasted_iota(jnp.int32, (ext, 2 * lanes), 0)
    lane_i = lax.broadcasted_iota(jnp.int32, (ext, 2 * lanes), 1)
    row_low = jnp.where(gx > 0, 0, RIM)
    row_high = jnp.where(gx < nx - 1, ext, RIM + rows)
    lane_low = jnp.where(gy < ny - 1, lanes + RIM, lanes)
    lane_high = jnp.where(gy > 0, 2 * lanes - RIM, 2 * lanes)
    valid = jnp.logical_and(
        jnp.logical_and(row_i >= row_low, row_i < row_high),
        jnp.logical_or(lane_i < lane_low, lane_i >= lane_high),
    )

    def field(i, fill):
        main = floats[i] if i < 8 else ints[i - 8].astype(jnp.float32)
        return jnp.where(valid, extend(i, main), fill)

    driving = field(0, 0.0)
    rate = field(1, 1.0)
    friction = field(2, 0.0)
    melt = field(3, 0.0)
    trans = field(4, 0.0)
    leakage = field(5, 1.0)
    pressure = field(6, 0.0)
    scale = field(7, 0.0)
    ice = field(8, 0.0)
    grounded = field(9, 0.0)
    friction = friction * grounded
    scale = scale * grounded

    w = basal_response()
    viscous = rate * float(FLOOR ** (-1.0 / 3.0))
    speed = driving / (4.0 * viscous)
    drop = -speed * friction / (viscous + friction * float(w[0]))
    speed = speed * ice
    drop = drop * ice
    sliding = speed + drop * float(w[0])
    squared = sliding * sliding
    trans_eff = trans * (1.0 + squared / (1.0 + squared))
    source = melt + HEATING * friction * squared
    pressure = water_solve(pressure, trans_eff, leakage, source, valid)
    friction = scale * pressure

    sxp, sxm, syp, sym = neighbours(speed)
    dxp, dxm, dyp, dym = neighbours(drop)
    sdx, sdy, ddx, ddy = sxp - sxm, syp - sym, dxp - dxm, dyp - dym
    flat = [
        0.03125 * (sdx * sdx + sdy * sdy) + 0.125 * FLOOR,
        0.0625 * (sdx * ddx + sdy * ddy),
        0.03125 * (ddx * ddx + ddy * ddy),
        0.125 * drop * drop,
        0.25 * ((sxp + sxm) + (syp + sym)),
        0.25 * ((dxp + dxm) + (dyp + dym)),
        driving * (0.5 / rate),
        friction * (0.5 / rate),
        ice,
    ]
    tall = rows + RIM
    tiles = tall // 8
    wide = 2 * RIM
    slot = lax.broadcasted_iota(jnp.int32, (8, lanes), 1) // wide

    def squeeze(f):
        f = turn(f, -HALF, 0)[:tall]
        tile = jnp.zeros((8, lanes), jnp.float32)
        for t in range(tiles):
            moved = turn(f[8 * t : 8 * t + 8, lanes:], wide * t + RIM, 1)
            tile = jnp.where(slot == t, moved, tile)
        return jnp.concatenate([f[:, :lanes], tile], axis=0)

    def spread(f):
        rim = [turn(f[tall:], -(wide * t + RIM), 1) for t in range(tiles)]
        whole = jnp.concatenate([f[:tall], jnp.concatenate(rim, axis=0)], axis=1)
        whole = jnp.concatenate([whole, jnp.zeros((RIM, 2 * lanes), jnp.float32)], axis=0)
        return turn(whole, HALF, 0)

    flat = [squeeze(f) for f in flat]
    for t in range(tiles + 1):
        at = slice(8 * t, 8 * t + 8)
        c0, c1, c2, c3, n0, n1, dr = [f[at] for f in flat[:7]]
        before = None
        for k in range(LAYERS):
            wk = float(w[k])
            strain = c0 + (c1 * wk + c2 * (wk * wk))
            if k < LAYERS - 1:
                strain = strain + c3 * float((w[k + 1] - w[k]) ** 2)
            twice = jnp.exp2(jnp.log(strain) * THIRD)
            q_ref[k, at] = twice
            r_ref[k, at] = dr + twice * (n0 + n1 * wk)
            if k > 0:
                g_ref[k - 1, at] = 0.5 * (before + twice)
            before = twice

    base = flat[7]
    up_d = None
    up_e, up_t = q_ref[0] + base, r_ref[0]
    down_d = None
    down_e, down_t = q_ref[LAYERS - 1], r_ref[LAYERS - 1]

    def step(d, e, t, g, q, r):
        d = e + (g if d is None else g * d)
        return d, q * d + g * e, r * d + g * t

    for k in range(LAYERS - 1):
        j = LAYERS - 2 - k
        up_d, up_e, up_t = step(up_d, up_e, up_t, g_ref[k], q_ref[k + 1], r_ref[k + 1])
        down_d, down_e, down_t = step(down_d, down_e, down_t, g_ref[j], q_ref[j], r_ref[j])
        if k % RESCALE == RESCALE - 1 and k < LAYERS - 2:
            shrink = 1.0 / up_d
            up_d, up_e, up_t = None, up_e * shrink, up_t * shrink
            shrink = 1.0 / down_d
            down_d, down_e, down_t = None, down_e * shrink, down_t * shrink
    surface = up_t / up_e * flat[8]
    basal = down_t / (down_e + base * down_d) * flat[8]

    sliding = jnp.where(valid, spread(basal), 0.0)
    squared = sliding * sliding
    trans_eff = trans * (1.0 + squared / (1.0 + squared))
    source = melt + HEATING * friction * squared
    pressure = water_solve(pressure, trans_eff, leakage, source, valid)
    block = pressure[RIM : RIM + rows, :lanes]
    send_p[...] = block

    def last():
        return pltpu.make_async_remote_copy(
            src_ref=send_p, dst_ref=out.at[0, strip], send_sem=last_send, recv_sem=last_recv.at[strip],
            device_id={"sec": sectors}, device_id_type=MESH,
        )

    @pl.when(sends_last)
    def _():
        last().start()

    @pl.when(is_ice)
    def _():
        out[0, 0] = turn(surface[:tall], -HALF, 0)[:rows]
        out[0, 1] = sliding[RIM : RIM + rows, :lanes]
        out[0, 2] = scale[RIM : RIM + rows, :lanes] * block

    @pl.when(jnp.logical_not(is_ice))
    def _():
        out[0, 0] = block

    for n in order:
        dx, dy = DIRECTIONS[n]

        @pl.when(exists(dx, dy))
        def _(dx=dx, dy=dy, n=n):
            for c in copies(dx, dy, n):
                c.wait_send()

    @pl.when(sends_last)
    def _():
        last().wait_send()

    for s in range(1, sectors):

        @pl.when(jnp.logical_not(is_ice))
        def _(s=s):
            pltpu.make_async_remote_copy(
                src_ref=send_p, dst_ref=out.at[0, s], send_sem=last_send, recv_sem=last_recv.at[s],
                device_id={"sec": 0}, device_id_type=MESH,
            ).wait_recv()


def on_device(nx, ny, *args):
    sectors, rows, lanes = args[0].shape
    ext = rows + 2 * RIM
    f32 = jnp.float32
    vmem = pltpu.VMEM
    dma = pltpu.SemaphoreType.DMA
    return pl.pallas_call(
        functools.partial(kernel, sectors, nx, ny),
        out_shape=jax.ShapeDtypeStruct((1, sectors, rows, lanes), f32),
        in_specs=[pl.BlockSpec(memory_space=pltpu.HBM)] * len(args),
        out_specs=pl.BlockSpec(memory_space=pltpu.VMEM),
        scratch_shapes=[
            vmem((8, ext, lanes), f32),
            vmem((2, ext, lanes), jnp.int32),
            vmem((rows, lanes), f32),
            vmem((rows, lanes), f32),
            vmem((ext, lanes), f32),
            vmem((ext, lanes), f32),
            vmem((LAYERS, ext, lanes), f32),
            vmem((LAYERS, ext, lanes), f32),
            vmem((LAYERS, ext, lanes), f32),
            vmem((rows, lanes), f32),
            dma((10,)),
            dma((16,)),
            dma((16,)),
            dma,
            dma((sectors,)),
        ],
        compiler_params=pltpu.CompilerParams(collective_id=0, has_side_effects=True),
    )(*args)


def solution(mesh):
    spec = P(None, "gx", "gy")
    return jax.shard_map(
        functools.partial(on_device, mesh.shape["gx"], mesh.shape["gy"]),
        mesh=mesh,
        in_specs=(spec,) * 10,
        out_specs=P("sec", None, "gx", "gy"),
        check_vma=False,
    )
```

```python
import functools

import jax
import jax.numpy as jnp
import numpy as np
from jax import lax
from jax.experimental import pallas as pl
from jax.experimental.pallas import tpu as pltpu
from jax.sharding import PartitionSpec as P

LAYERS = 40
SWEEPS = 4
VERT = 4.0
FLOOR = 0.25
HEATING = 0.5

RIM = 8
HALF = RIM // 2
RESCALE = 10
THIRD = -1.0 / (3.0 * float(np.log(2.0)))
DIRECTIONS = [(dx, dy) for dx in (-1, 0, 1) for dy in (-1, 0, 1) if (dx, dy) != (0, 0)]
MESH = pl.DeviceIdType.MESH


def basal_response():
    matrix = np.zeros((LAYERS, LAYERS))
    for k in range(LAYERS):
        matrix[k, k] = 4.0 + (VERT if k > 0 else 0.0) + (VERT if k < LAYERS - 1 else 0.0)
        if k > 0:
            matrix[k, k - 1] = matrix[k - 1, k] = -VERT
    unit = np.zeros(LAYERS)
    unit[0] = 1.0
    return np.linalg.solve(matrix, unit)


def turn(values, shift, axis):
    return pltpu.roll(values, shift % values.shape[axis], axis)


def neighbours(f):
    return turn(f, -1, 0), turn(f, 1, 0), turn(f, -1, 1), turn(f, 1, 1)


def water_solve(pressure, trans_eff, leakage, source, valid):
    faces = [0.5 * (trans_eff + t) for t in neighbours(trans_eff)]
    total = leakage + ((faces[0] + faces[1]) + (faces[2] + faces[3]))
    inverse = jnp.where(valid, 1.0 / total, 0.0)
    weights = [f * inverse for f in faces]
    base = source * inverse
    for _ in range(SWEEPS):
        parts = [w * p for w, p in zip(weights, neighbours(pressure))]
        pressure = base + ((parts[0] + parts[1]) + (parts[2] + parts[3]))
    return pressure


def kernel(sectors, nx, ny, *refs):
    ins = refs[:10]
    out = refs[10]
    floats, ints, pack_l, pack_r, rim_l, rim_r, q_ref, g_ref, r_ref, send_p = refs[11:21]
    in_sem, send_sem, recv_sem, last_send, last_recv = refs[21:]
    rows, lanes = ins[0].shape[1:]
    sec = lax.axis_index("sec")
    gx = lax.axis_index("gx")
    gy = lax.axis_index("gy")
    strip = lax.rem(sec, sectors)
    is_ice = sec < sectors
    sends_last = jnp.logical_and(sec > 0, is_ice)

    def exists(dx, dy):
        x, y = gx + dx, gy + dy
        return jnp.logical_and(
            jnp.logical_and(x >= 0, x < nx), jnp.logical_and(y >= 0, y < ny)
        )

    float_ids = (0, 1, 2, 5, 6, 7, 8, 9)
    int_ids = (3, 4)
    loads = []
    for slot, arg in enumerate(float_ids):
        loads.append(pltpu.make_async_copy(ins[arg].at[strip], floats.at[slot, pl.ds(RIM, rows)], in_sem.at[slot]))
    for slot, arg in enumerate(int_ids):
        loads.append(pltpu.make_async_copy(ins[arg].at[strip], ints.at[slot, pl.ds(RIM, rows)], in_sem.at[8 + slot]))
    for load in loads:
        load.start()

    barrier = pltpu.get_barrier_semaphore()
    count = jnp.int32(0)
    for dx, dy in DIRECTIONS:
        here = exists(dx, dy)
        count = count + here.astype(jnp.int32)

        @pl.when(here)
        def _(dx=dx, dy=dy):
            pl.semaphore_signal(barrier, inc=1, device_id={"gx": gx + dx, "gy": gy + dy}, device_id_type=MESH)

    count = count + sends_last.astype(jnp.int32)
    count = count + jnp.where(is_ice, 0, sectors - 1)

    @pl.when(sends_last)
    def _():
        pl.semaphore_signal(barrier, inc=1, device_id={"sec": sectors}, device_id_type=MESH)

    for s in range(1, sectors):

        @pl.when(jnp.logical_not(is_ice))
        def _(s=s):
            pl.semaphore_signal(barrier, inc=1, device_id={"sec": s}, device_id_type=MESH)

    for load in loads:
        load.wait()

    lane = lax.broadcasted_iota(jnp.int32, (rows, lanes), 1)
    fields = [floats[i, RIM : RIM + rows] for i in range(8)]
    fields += [ints[i, RIM : RIM + rows].astype(jnp.float32) for i in range(2)]
    left = jnp.zeros((rows, lanes), jnp.float32)
    right = jnp.zeros((rows, lanes), jnp.float32)
    for i, f in enumerate(fields):
        moved = turn(f, RIM * i, 1)
        group = lane // RIM
        left = jnp.where(group == i, moved, left)
        right = jnp.where(group == (i - 1) % (lanes // RIM), moved, right)
    pack_l[...] = left
    pack_r[...] = right

    pl.semaphore_wait(barrier, count)

    def copies(dx, dy, n):
        target = {"gx": gx + dx, "gy": gy + dy}

        def remote(src, dst, m):
            return pltpu.make_async_remote_copy(
                src_ref=src, dst_ref=dst, send_sem=send_sem.at[m], recv_sem=recv_sem.at[m],
                device_id=target, device_id_type=MESH,
            )

        if dy == 0:
            first = rows if dx > 0 else RIM
            landing = 0 if dx > 0 else RIM + rows
            return [
                remote(floats.at[:, pl.ds(first, RIM)], floats.at[:, pl.ds(landing, RIM)], n),
                remote(ints.at[:, pl.ds(first, RIM)], ints.at[:, pl.ds(landing, RIM)], n + 8),
            ]
        src, dst = (pack_r, rim_l) if dy > 0 else (pack_l, rim_r)
        if dx == 0:
            return [remote(src, dst.at[pl.ds(RIM, rows)], n)]
        first = rows - RIM if dx > 0 else 0
        landing = 0 if dx > 0 else RIM + rows
        return [remote(src.at[pl.ds(first, RIM)], dst.at[pl.ds(landing, RIM)], n)]

    order = sorted(range(8), key=lambda n: abs(DIRECTIONS[n][1]))
    for n in order:
        dx, dy = DIRECTIONS[n]

        @pl.when(exists(dx, dy))
        def _(dx=dx, dy=dy, n=n):
            for c in copies(dx, dy, n):
                c.start()

    for n in order:
        dx, dy = DIRECTIONS[n]

        @pl.when(exists(-dx, -dy))
        def _(dx=dx, dy=dy, n=n):
            for c in copies(dx, dy, n):
                c.wait_recv()

    ext = rows + 2 * RIM
    group = lax.broadcasted_iota(jnp.int32, (ext, lanes), 1) // RIM
    packed_l = rim_l[...]
    packed_r = rim_r[...]

    def extend(i, main):
        rim = turn(jnp.where(group == i, packed_r, packed_l), -RIM * i, 1)
        return jnp.concatenate([main, rim], axis=1)

    row_i = lax.broadcasted_iota(jnp.int32, (ext, 2 * lanes), 0)
    lane_i = lax.broadcasted_iota(jnp.int32, (ext, 2 * lanes), 1)
    row_low = jnp.where(gx > 0, 0, RIM)
    row_high = jnp.where(gx < nx - 1, ext, RIM + rows)
    lane_low = jnp.where(gy < ny - 1, lanes + RIM, lanes)
    lane_high = jnp.where(gy > 0, 2 * lanes - RIM, 2 * lanes)
    valid = jnp.logical_and(
        jnp.logical_and(row_i >= row_low, row_i < row_high),
        jnp.logical_or(lane_i < lane_low, lane_i >= lane_high),
    )

    def field(i, fill):
        main = floats[i] if i < 8 else ints[i - 8].astype(jnp.float32)
        return jnp.where(valid, extend(i, main), fill)

    driving = field(0, 0.0)
    rate = field(1, 1.0)
    friction = field(2, 0.0)
    melt = field(3, 0.0)
    trans = field(4, 0.0)
    leakage = field(5, 1.0)
    pressure = field(6, 0.0)
    scale = field(7, 0.0)
    ice = field(8, 0.0)
    grounded = field(9, 0.0)
    friction = friction * grounded
    scale = scale * grounded

    w = basal_response()
    viscous = rate * float(FLOOR ** (-1.0 / 3.0))
    speed = driving / (4.0 * viscous)
    drop = -speed * friction / (viscous + friction * float(w[0]))
    speed = speed * ice
    drop = drop * ice
    sliding = speed + drop * float(w[0])
    squared = sliding * sliding
    trans_eff = trans * (1.0 + squared / (1.0 + squared))
    source = melt + HEATING * friction * squared
    pressure = water_solve(pressure, trans_eff, leakage, source, valid)
    friction = scale * pressure

    sxp, sxm, syp, sym = neighbours(speed)
    dxp, dxm, dyp, dym = neighbours(drop)
    sdx, sdy, ddx, ddy = sxp - sxm, syp - sym, dxp - dxm, dyp - dym
    flat = [
        0.03125 * (sdx * sdx + sdy * sdy) + 0.125 * FLOOR,
        0.0625 * (sdx * ddx + sdy * ddy),
        0.03125 * (ddx * ddx + ddy * ddy),
        0.125 * drop * drop,
        0.25 * ((sxp + sxm) + (syp + sym)),
        0.25 * ((dxp + dxm) + (dyp + dym)),
        driving * (0.5 / rate),
        friction * (0.5 / rate),
        ice,
    ]
    tall = rows + RIM
    tiles = tall // 8
    wide = 2 * RIM
    slot = lax.broadcasted_iota(jnp.int32, (8, lanes), 1) // wide

    def squeeze(f):
        f = turn(f, -HALF, 0)[:tall]
        tile = jnp.zeros((8, lanes), jnp.float32)
        for t in range(tiles):
            moved = turn(f[8 * t : 8 * t + 8, lanes:], wide * t + RIM, 1)
            tile = jnp.where(slot == t, moved, tile)
        return jnp.concatenate([f[:, :lanes], tile], axis=0)

    def spread(f):
        rim = [turn(f[tall:], -(wide * t + RIM), 1) for t in range(tiles)]
        whole = jnp.concatenate([f[:tall], jnp.concatenate(rim, axis=0)], axis=1)
        whole = jnp.concatenate([whole, jnp.zeros((RIM, 2 * lanes), jnp.float32)], axis=0)
        return turn(whole, HALF, 0)

    flat = [squeeze(f) for f in flat]
    for t in range(tiles + 1):
        at = slice(8 * t, 8 * t + 8)
        c0, c1, c2, c3, n0, n1, dr = [f[at] for f in flat[:7]]
        before = None
        for k in range(LAYERS):
            wk = float(w[k])
            strain = c0 + (c1 * wk + c2 * (wk * wk))
            if k < LAYERS - 1:
                strain = strain + c3 * float((w[k + 1] - w[k]) ** 2)
            twice = jnp.exp2(jnp.log(strain) * THIRD)
            q_ref[k, at] = twice
            r_ref[k, at] = dr + twice * (n0 + n1 * wk)
            if k > 0:
                g_ref[k - 1, at] = 0.5 * (before + twice)
            before = twice

    base = flat[7]
    up_d = None
    up_e, up_t = q_ref[0] + base, r_ref[0]
    down_d = None
    down_e, down_t = q_ref[LAYERS - 1], r_ref[LAYERS - 1]

    def step(d, e, t, g, q, r):
        d = e + (g if d is None else g * d)
        return d, q * d + g * e, r * d + g * t

    for k in range(LAYERS - 1):
        j = LAYERS - 2 - k
        up_d, up_e, up_t = step(up_d, up_e, up_t, g_ref[k], q_ref[k + 1], r_ref[k + 1])
        down_d, down_e, down_t = step(down_d, down_e, down_t, g_ref[j], q_ref[j], r_ref[j])
        if k % RESCALE == RESCALE - 1 and k < LAYERS - 2:
            shrink = 1.0 / up_d
            up_d, up_e, up_t = None, up_e * shrink, up_t * shrink
            shrink = 1.0 / down_d
            down_d, down_e, down_t = None, down_e * shrink, down_t * shrink
    surface = up_t / up_e * flat[8]
    basal = down_t / (down_e + base * down_d) * flat[8]

    sliding = jnp.where(valid, spread(basal), 0.0)
    squared = sliding * sliding
    trans_eff = trans * (1.0 + squared / (1.0 + squared))
    source = melt + HEATING * friction * squared
    pressure = water_solve(pressure, trans_eff, leakage, source, valid)
    block = pressure[RIM : RIM + rows, :lanes]
    send_p[...] = block

    def last():
        return pltpu.make_async_remote_copy(
            src_ref=send_p, dst_ref=out.at[0, strip], send_sem=last_send, recv_sem=last_recv.at[strip],
            device_id={"sec": sectors}, device_id_type=MESH,
        )

    @pl.when(sends_last)
    def _():
        last().start()

    @pl.when(is_ice)
    def _():
        out[0, 0] = turn(surface[:tall], -HALF, 0)[:rows]
        out[0, 1] = sliding[RIM : RIM + rows, :lanes]
        out[0, 2] = scale[RIM : RIM + rows, :lanes] * block

    @pl.when(jnp.logical_not(is_ice))
    def _():
        out[0, 0] = block

    for n in order:
        dx, dy = DIRECTIONS[n]

        @pl.when(exists(dx, dy))
        def _(dx=dx, dy=dy, n=n):
            for c in copies(dx, dy, n):
                c.wait_send()

    @pl.when(sends_last)
    def _():
        last().wait_send()

    for s in range(1, sectors):

        @pl.when(jnp.logical_not(is_ice))
        def _(s=s):
            pltpu.make_async_remote_copy(
                src_ref=send_p, dst_ref=out.at[0, s], send_sem=last_send, recv_sem=last_recv.at[s],
                device_id={"sec": 0}, device_id_type=MESH,
            ).wait_recv()


def on_device(nx, ny, *args):
    sectors, rows, lanes = args[0].shape
    ext = rows + 2 * RIM
    f32 = jnp.float32
    vmem = pltpu.VMEM
    dma = pltpu.SemaphoreType.DMA
    return pl.pallas_call(
        functools.partial(kernel, sectors, nx, ny),
        out_shape=pltpu.VMEM((1, sectors, rows, lanes), f32),
        in_specs=[pl.BlockSpec(memory_space=pltpu.HBM)] * len(args),
        out_specs=pl.BlockSpec(memory_space=pltpu.VMEM),
        scratch_shapes=[
            vmem((8, ext, lanes), f32),
            vmem((2, ext, lanes), jnp.int32),
            vmem((rows, lanes), f32),
            vmem((rows, lanes), f32),
            vmem((ext, lanes), f32),
            vmem((ext, lanes), f32),
            vmem((LAYERS, ext, lanes), f32),
            vmem((LAYERS, ext, lanes), f32),
            vmem((LAYERS, ext, lanes), f32),
            vmem((rows, lanes), f32),
            dma((10,)),
            dma((16,)),
            dma((16,)),
            dma,
            dma((sectors,)),
        ],
        compiler_params=pltpu.CompilerParams(collective_id=0, has_side_effects=True),
    )(*args)


def solution(mesh):
    spec = P(None, "gx", "gy")
    return jax.shard_map(
        functools.partial(on_device, mesh.shape["gx"], mesh.shape["gy"]),
        mesh=mesh,
        in_specs=(spec,) * 10,
        out_specs=P("sec", None, "gx", "gy"),
        check_vma=False,
    )
```

```python
import functools

import jax
import jax.numpy as jnp
import numpy as np
from jax import lax
from jax.experimental import pallas as pl
from jax.experimental.pallas import tpu as pltpu
from jax.sharding import PartitionSpec as P

LAYERS = 40
SWEEPS = 4
VERT = 4.0
FLOOR = 0.25
HEATING = 0.5

RIM = 8
HALF = RIM // 2
RESCALE = 10
THIRD = -1.0 / (3.0 * float(np.log(2.0)))
DIRECTIONS = [(dx, dy) for dx in (-1, 0, 1) for dy in (-1, 0, 1) if (dx, dy) != (0, 0)]
MESH = pl.DeviceIdType.MESH


def basal_response():
    matrix = np.zeros((LAYERS, LAYERS))
    for k in range(LAYERS):
        matrix[k, k] = 4.0 + (VERT if k > 0 else 0.0) + (VERT if k < LAYERS - 1 else 0.0)
        if k > 0:
            matrix[k, k - 1] = matrix[k - 1, k] = -VERT
    unit = np.zeros(LAYERS)
    unit[0] = 1.0
    return np.linalg.solve(matrix, unit)


def turn(values, shift, axis):
    return pltpu.roll(values, shift % values.shape[axis], axis)


def neighbours(f):
    return turn(f, -1, 0), turn(f, 1, 0), turn(f, -1, 1), turn(f, 1, 1)


def water_solve(pressure, trans_eff, leakage, source, valid):
    faces = [0.5 * (trans_eff + t) for t in neighbours(trans_eff)]
    total = leakage + ((faces[0] + faces[1]) + (faces[2] + faces[3]))
    inverse = jnp.where(valid, 1.0 / total, 0.0)
    weights = [f * inverse for f in faces]
    base = source * inverse
    for _ in range(SWEEPS):
        parts = [w * p for w, p in zip(weights, neighbours(pressure))]
        pressure = base + ((parts[0] + parts[1]) + (parts[2] + parts[3]))
    return pressure


def kernel(sectors, nx, ny, *refs):
    ins = refs[:10]
    out = refs[10]
    floats, ints, pack_l, pack_r, rim_l, rim_r, q_ref, g_ref, r_ref, send_p = refs[11:21]
    in_sem, send_sem, recv_sem, last_send, last_recv = refs[21:]
    rows, lanes = ins[0].shape[1:]
    sec = lax.axis_index("sec")
    gx = lax.axis_index("gx")
    gy = lax.axis_index("gy")
    strip = lax.rem(sec, sectors)
    is_ice = sec < sectors
    sends_last = jnp.logical_and(sec > 0, is_ice)

    def exists(dx, dy):
        x, y = gx + dx, gy + dy
        return jnp.logical_and(
            jnp.logical_and(x >= 0, x < nx), jnp.logical_and(y >= 0, y < ny)
        )

    float_ids = (0, 1, 2, 5, 6, 7, 8, 9)
    int_ids = (3, 4)
    loads = []
    for slot, arg in enumerate(float_ids):
        loads.append(pltpu.make_async_copy(ins[arg].at[strip], floats.at[slot, pl.ds(RIM, rows)], in_sem.at[slot]))
    for slot, arg in enumerate(int_ids):
        loads.append(pltpu.make_async_copy(ins[arg].at[strip], ints.at[slot, pl.ds(RIM, rows)], in_sem.at[8 + slot]))
    for load in loads:
        load.start()

    barrier = pltpu.get_barrier_semaphore()
    count = jnp.int32(0)
    for dx, dy in DIRECTIONS:
        here = exists(dx, dy)
        count = count + here.astype(jnp.int32)

        @pl.when(here)
        def _(dx=dx, dy=dy):
            pl.semaphore_signal(barrier, inc=1, device_id={"gx": gx + dx, "gy": gy + dy}, device_id_type=MESH)

    count = count + sends_last.astype(jnp.int32)
    count = count + jnp.where(is_ice, 0, sectors - 1)

    @pl.when(sends_last)
    def _():
        pl.semaphore_signal(barrier, inc=1, device_id={"sec": sectors}, device_id_type=MESH)

    for s in range(1, sectors):

        @pl.when(jnp.logical_not(is_ice))
        def _(s=s):
            pl.semaphore_signal(barrier, inc=1, device_id={"sec": s}, device_id_type=MESH)

    for load in loads:
        load.wait()

    lane = lax.broadcasted_iota(jnp.int32, (rows, lanes), 1)
    fields = [floats[i, RIM : RIM + rows] for i in range(8)]
    fields += [ints[i, RIM : RIM + rows].astype(jnp.float32) for i in range(2)]
    left = jnp.zeros((rows, lanes), jnp.float32)
    right = jnp.zeros((rows, lanes), jnp.float32)
    for i, f in enumerate(fields):
        moved = turn(f, RIM * i, 1)
        group = lane // RIM
        left = jnp.where(group == i, moved, left)
        right = jnp.where(group == (i - 1) % (lanes // RIM), moved, right)
    pack_l[...] = left
    pack_r[...] = right

    pl.semaphore_wait(barrier, count)

    def copies(dx, dy, n):
        target = {"gx": gx + dx, "gy": gy + dy}

        def remote(src, dst, m):
            return pltpu.make_async_remote_copy(
                src_ref=src, dst_ref=dst, send_sem=send_sem.at[m], recv_sem=recv_sem.at[m],
                device_id=target, device_id_type=MESH,
            )

        if dy == 0:
            first = rows if dx > 0 else RIM
            landing = 0 if dx > 0 else RIM + rows
            return [
                remote(floats.at[:, pl.ds(first, RIM)], floats.at[:, pl.ds(landing, RIM)], n),
                remote(ints.at[:, pl.ds(first, RIM)], ints.at[:, pl.ds(landing, RIM)], n + 8),
            ]
        src, dst = (pack_r, rim_l) if dy > 0 else (pack_l, rim_r)
        if dx == 0:
            return [remote(src, dst.at[pl.ds(RIM, rows)], n)]
        first = rows - RIM if dx > 0 else 0
        landing = 0 if dx > 0 else RIM + rows
        return [remote(src.at[pl.ds(first, RIM)], dst.at[pl.ds(landing, RIM)], n)]

    order = sorted(range(8), key=lambda n: abs(DIRECTIONS[n][1]))
    for n in order:
        dx, dy = DIRECTIONS[n]

        @pl.when(exists(dx, dy))
        def _(dx=dx, dy=dy, n=n):
            for c in copies(dx, dy, n):
                c.start()

    def arrive(n):
        dx, dy = DIRECTIONS[n]

        @pl.when(exists(-dx, -dy))
        def _():
            for c in copies(dx, dy, n):
                c.wait_recv()

    w = basal_response()
    ext = rows + 2 * RIM
    tall = rows + RIM
    tiles = tall // 8
    wide = 2 * RIM
    slot = lax.broadcasted_iota(jnp.int32, (8, lanes), 1) // wide
    lane_low = jnp.where(gy < ny - 1, lanes + RIM, lanes)
    lane_high = jnp.where(gy > 0, 2 * lanes - RIM, 2 * lanes)

    def in_map_lanes(height):
        lane_i = lax.broadcasted_iota(jnp.int32, (height, 2 * lanes), 1)
        return jnp.logical_or(lane_i < lane_low, lane_i >= lane_high)

    def field_reader(top, height, valid):
        at = slice(top, top + height)
        packed_l, packed_r = rim_l[at], rim_r[at]
        group = lax.broadcasted_iota(jnp.int32, (height, lanes), 1) // RIM

        def field(i, fill):
            main = floats[i, at] if i < 8 else ints[i - 8, at].astype(jnp.float32)
            rim = turn(jnp.where(group == i, packed_r, packed_l), -RIM * i, 1)
            return jnp.where(valid, jnp.concatenate([main, rim], axis=1), fill)

        return field

    def first_velocity(driving, rate, friction, ice):
        viscous = rate * float(FLOOR ** (-1.0 / 3.0))
        speed = driving / (4.0 * viscous)
        drop = -speed * friction / (viscous + friction * float(w[0]))
        return speed * ice, drop * ice

    def squeeze(f, which):
        tile = jnp.zeros((8, lanes), jnp.float32)
        for n, t in enumerate(which):
            moved = turn(f[8 * t : 8 * t + 8, lanes:], wide * n + RIM, 1)
            tile = jnp.where(slot == n, moved, tile)
        return jnp.concatenate([f[8 * t : 8 * t + 8, :lanes] for t in which] + [tile], axis=0)

    def spread(f, count):
        last = f[8 * count :]
        return [
            jnp.concatenate([f[8 * n : 8 * n + 8], turn(last, -(wide * n + RIM), 1)], axis=1)
            for n in range(count)
        ]

    def eliminate(speed, drop, driving, rate, which, offset, lead):
        sxp, sxm, syp, sym = neighbours(speed)
        dxp, dxm, dyp, dym = neighbours(drop)
        sdx, sdy, ddx, ddy = sxp - sxm, syp - sym, dxp - dxm, dyp - dym
        flat = [
            0.03125 * (sdx * sdx + sdy * sdy) + 0.125 * FLOOR,
            0.0625 * (sdx * ddx + sdy * ddy),
            0.03125 * (ddx * ddx + ddy * ddy),
            0.125 * drop * drop,
            0.25 * ((sxp + sxm) + (syp + sym)),
            0.25 * ((dxp + dxm) + (dyp + dym)),
            driving * (0.5 / rate),
        ]
        flat = [squeeze(turn(f, lead, 0), which) for f in flat]
        for n in range(len(which) + 1):
            at = slice(offset + 8 * n, offset + 8 * n + 8)
            c0, c1, c2, c3, n0, n1, dr = [f[8 * n : 8 * n + 8] for f in flat]
            before = None
            for k in range(LAYERS):
                wk = float(w[k])
                strain = c0 + (c1 * wk + c2 * (wk * wk))
                if k < LAYERS - 1:
                    strain = strain + c3 * float((w[k + 1] - w[k]) ** 2)
                twice = jnp.exp2(jnp.log(strain) * THIRD)
                q_ref[k, at] = twice
                r_ref[k, at] = dr + twice * (n0 + n1 * wk)
                if k > 0:
                    g_ref[k - 1, at] = 0.5 * (before + twice)
                before = twice

        at = slice(offset, offset + 8 * (len(which) + 1))
        up_d, up_e, up_t = None, q_ref[0, at], r_ref[0, at]
        down_d, down_e, down_t = None, q_ref[LAYERS - 1, at], r_ref[LAYERS - 1, at]
        product = None

        def step(d, e, t, g, q, r):
            d = e + (g if d is None else g * d)
            return d, q * d + g * e, r * d + g * t

        for k in range(LAYERS - 1):
            j = LAYERS - 2 - k
            g = g_ref[k, at]
            product = g if product is None else product * g
            up_d, up_e, up_t = step(up_d, up_e, up_t, g, q_ref[k + 1, at], r_ref[k + 1, at])
            down_d, down_e, down_t = step(
                down_d, down_e, down_t, g_ref[j, at], q_ref[j, at], r_ref[j, at]
            )
            if k % RESCALE == RESCALE - 1 and k < LAYERS - 2:
                shrink = 1.0 / up_d
                up_d, up_e, up_t, product = None, up_e * shrink, up_t * shrink, product * shrink
                shrink = 1.0 / down_d
                down_d, down_e, down_t = None, down_e * shrink, down_t * shrink
        shrink = 1.0 / up_e
        return down_d, down_e, down_t, up_t * shrink, product * shrink

    def finish(parts, friction, rate, ice, which):
        down_d, down_e, down_t, top, reach = parts
        base = squeeze(turn(friction * (0.5 / rate), -HALF, 0), which)
        mask = squeeze(turn(ice, -HALF, 0), which)
        basal = down_t / (down_e + base * down_d)
        surface = top - base * basal * reach
        return [spread(f * mask, len(which)) for f in (basal, surface)]

    for n in order:
        if DIRECTIONS[n][0] == 0:
            arrive(n)
    early = list(range(1, tiles - 1))
    late = [0, tiles - 1]
    field = field_reader(RIM, rows, in_map_lanes(rows))
    driving, rate = field(0, 0.0), field(1, 1.0)
    speed, drop = first_velocity(driving, rate, field(2, 0.0) * field(9, 0.0), field(8, 0.0))
    early_parts = eliminate(speed, drop, driving, rate, early, 0, HALF)
    for n in order:
        if DIRECTIONS[n][0] != 0:
            arrive(n)

    row_i = lax.broadcasted_iota(jnp.int32, (ext, 2 * lanes), 0)
    row_low = jnp.where(gx > 0, 0, RIM)
    row_high = jnp.where(gx < nx - 1, ext, RIM + rows)
    valid = jnp.logical_and(
        jnp.logical_and(row_i >= row_low, row_i < row_high), in_map_lanes(ext)
    )
    field = field_reader(0, ext, valid)
    driving = field(0, 0.0)
    rate = field(1, 1.0)
    friction = field(2, 0.0)
    melt = field(3, 0.0)
    trans = field(4, 0.0)
    leakage = field(5, 1.0)
    pressure = field(6, 0.0)
    scale = field(7, 0.0)
    ice = field(8, 0.0)
    grounded = field(9, 0.0)
    friction = friction * grounded
    scale = scale * grounded

    speed, drop = first_velocity(driving, rate, friction, ice)
    sliding = speed + drop * float(w[0])
    squared = sliding * sliding
    trans_eff = trans * (1.0 + squared / (1.0 + squared))
    source = melt + HEATING * friction * squared
    pressure = water_solve(pressure, trans_eff, leakage, source, valid)
    friction = scale * pressure

    late_parts = eliminate(speed, drop, driving, rate, late, 8 * (len(early) + 1), -HALF)
    pieces = [None] * tiles
    for parts, which in ((early_parts, early), (late_parts, late)):
        for n, piece in enumerate(zip(*finish(parts, friction, rate, ice, which))):
            pieces[which[n]] = piece
    blank = jnp.zeros((RIM, 2 * lanes), jnp.float32)
    basal = turn(jnp.concatenate([p[0] for p in pieces] + [blank], axis=0), HALF, 0)
    surface = jnp.concatenate([p[1][:, :lanes] for p in pieces], axis=0)
    sliding = jnp.where(valid, basal, 0.0)
    squared = sliding * sliding
    trans_eff = trans * (1.0 + squared / (1.0 + squared))
    source = melt + HEATING * friction * squared
    pressure = water_solve(pressure, trans_eff, leakage, source, valid)
    block = pressure[RIM : RIM + rows, :lanes]
    send_p[...] = block

    def last():
        return pltpu.make_async_remote_copy(
            src_ref=send_p, dst_ref=out.at[0, strip], send_sem=last_send, recv_sem=last_recv.at[strip],
            device_id={"sec": sectors}, device_id_type=MESH,
        )

    @pl.when(sends_last)
    def _():
        last().start()

    @pl.when(is_ice)
    def _():
        out[0, 0] = turn(surface, -HALF, 0)[:rows]
        out[0, 1] = sliding[RIM : RIM + rows, :lanes]
        out[0, 2] = scale[RIM : RIM + rows, :lanes] * block

    @pl.when(jnp.logical_not(is_ice))
    def _():
        out[0, 0] = block

    for n in order:
        dx, dy = DIRECTIONS[n]

        @pl.when(exists(dx, dy))
        def _(dx=dx, dy=dy, n=n):
            for c in copies(dx, dy, n):
                c.wait_send()

    @pl.when(sends_last)
    def _():
        last().wait_send()

    for s in range(1, sectors):

        @pl.when(jnp.logical_not(is_ice))
        def _(s=s):
            pltpu.make_async_remote_copy(
                src_ref=send_p, dst_ref=out.at[0, s], send_sem=last_send, recv_sem=last_recv.at[s],
                device_id={"sec": 0}, device_id_type=MESH,
            ).wait_recv()


def on_device(nx, ny, *args):
    sectors, rows, lanes = args[0].shape
    ext = rows + 2 * RIM
    f32 = jnp.float32
    vmem = pltpu.VMEM
    dma = pltpu.SemaphoreType.DMA
    return pl.pallas_call(
        functools.partial(kernel, sectors, nx, ny),
        out_shape=pltpu.VMEM((1, sectors, rows, lanes), f32),
        in_specs=[pl.BlockSpec(memory_space=pltpu.HBM)] * len(args),
        out_specs=pl.BlockSpec(memory_space=pltpu.VMEM),
        scratch_shapes=[
            vmem((8, ext, lanes), f32),
            vmem((2, ext, lanes), jnp.int32),
            vmem((rows, lanes), f32),
            vmem((rows, lanes), f32),
            vmem((ext, lanes), f32),
            vmem((ext, lanes), f32),
            vmem((LAYERS, ext + RIM, lanes), f32),
            vmem((LAYERS, ext + RIM, lanes), f32),
            vmem((LAYERS, ext + RIM, lanes), f32),
            vmem((rows, lanes), f32),
            dma((10,)),
            dma((16,)),
            dma((16,)),
            dma,
            dma((sectors,)),
        ],
        compiler_params=pltpu.CompilerParams(collective_id=0, has_side_effects=True),
    )(*args)


def solution(mesh):
    spec = P(None, "gx", "gy")
    return jax.shard_map(
        functools.partial(on_device, mesh.shape["gx"], mesh.shape["gy"]),
        mesh=mesh,
        in_specs=(spec,) * 10,
        out_specs=P("sec", None, "gx", "gy"),
        check_vma=False,
    )
```

```python
import functools

import jax
import jax.numpy as jnp
import numpy as np
from jax import lax
from jax.experimental import pallas as pl
from jax.experimental.pallas import tpu as pltpu
from jax.sharding import PartitionSpec as P

LAYERS = 40
SWEEPS = 4
VERT = 4.0
FLOOR = 0.25
HEATING = 0.5

RIM = 8
HALF = RIM // 2
RESCALE = 10
THIRD = -1.0 / (3.0 * float(np.log(2.0)))
DIRECTIONS = [(dx, dy) for dx in (-1, 0, 1) for dy in (-1, 0, 1) if (dx, dy) != (0, 0)]
MESH = pl.DeviceIdType.MESH


def basal_response():
    matrix = np.zeros((LAYERS, LAYERS))
    for k in range(LAYERS):
        matrix[k, k] = 4.0 + (VERT if k > 0 else 0.0) + (VERT if k < LAYERS - 1 else 0.0)
        if k > 0:
            matrix[k, k - 1] = matrix[k - 1, k] = -VERT
    unit = np.zeros(LAYERS)
    unit[0] = 1.0
    return np.linalg.solve(matrix, unit)


def turn(values, shift, axis):
    return pltpu.roll(values, shift % values.shape[axis], axis)


def neighbours(f):
    return turn(f, -1, 0), turn(f, 1, 0), turn(f, -1, 1), turn(f, 1, 1)


def water_solve(pressure, trans_eff, leakage, source, valid):
    faces = [0.5 * (trans_eff + t) for t in neighbours(trans_eff)]
    total = leakage + ((faces[0] + faces[1]) + (faces[2] + faces[3]))
    inverse = jnp.where(valid, 1.0 / total, 0.0)
    weights = [f * inverse for f in faces]
    base = source * inverse
    for _ in range(SWEEPS):
        parts = [w * p for w, p in zip(weights, neighbours(pressure))]
        pressure = base + ((parts[0] + parts[1]) + (parts[2] + parts[3]))
    return pressure


def kernel(sectors, nx, ny, *refs):
    ins = refs[:10]
    out = refs[10]
    floats, ints, pack_l, pack_r, rim_l, rim_r, q_ref, g_ref, r_ref, send_p = refs[11:21]
    in_sem, send_sem, recv_sem, last_send, last_recv = refs[21:]
    rows, lanes = ins[0].shape[1:]
    sec = lax.axis_index("sec")
    gx = lax.axis_index("gx")
    gy = lax.axis_index("gy")
    strip = lax.rem(sec, sectors)
    is_ice = sec < sectors
    sends_last = jnp.logical_and(sec > 0, is_ice)

    def exists(dx, dy):
        x, y = gx + dx, gy + dy
        return jnp.logical_and(
            jnp.logical_and(x >= 0, x < nx), jnp.logical_and(y >= 0, y < ny)
        )

    float_ids = (0, 1, 2, 5, 6, 7, 8, 9)
    int_ids = (3, 4)
    loads = []
    for slot, arg in enumerate(float_ids):
        loads.append(pltpu.make_async_copy(ins[arg].at[strip], floats.at[slot, pl.ds(RIM, rows)], in_sem.at[0]))
    for slot, arg in enumerate(int_ids):
        loads.append(pltpu.make_async_copy(ins[arg].at[strip], ints.at[slot, pl.ds(RIM, rows)], in_sem.at[1]))
    barrier = pltpu.get_barrier_semaphore()
    count = jnp.int32(0)
    for dx, dy in sorted(DIRECTIONS, key=lambda d: -abs(d[0])):
        here = exists(dx, dy)
        count = count + here.astype(jnp.int32)

        @pl.when(here)
        def _(dx=dx, dy=dy):
            pl.semaphore_signal(barrier, inc=1, device_id={"gx": gx + dx, "gy": gy + dy}, device_id_type=MESH)

    count = count + sends_last.astype(jnp.int32)
    count = count + jnp.where(is_ice, 0, sectors - 1)

    @pl.when(sends_last)
    def _():
        pl.semaphore_signal(barrier, inc=1, device_id={"sec": sectors}, device_id_type=MESH)

    for s in range(1, sectors):

        @pl.when(jnp.logical_not(is_ice))
        def _(s=s):
            pl.semaphore_signal(barrier, inc=1, device_id={"sec": s}, device_id_type=MESH)

    for load in loads:
        load.start()
    for slot, buffer in enumerate((floats, ints)):
        mine = buffer.at[:, pl.ds(RIM, rows)]
        pltpu.make_async_copy(mine, mine, in_sem.at[slot]).wait()

    lane = lax.broadcasted_iota(jnp.int32, (rows, lanes), 1)
    fields = [floats[i, RIM : RIM + rows] for i in range(8)]
    fields += [ints[i, RIM : RIM + rows].astype(jnp.float32) for i in range(2)]
    left = jnp.zeros((rows, lanes), jnp.float32)
    right = jnp.zeros((rows, lanes), jnp.float32)
    for i, f in enumerate(fields):
        moved = turn(f, RIM * i, 1)
        group = lane // RIM
        left = jnp.where(group == i, moved, left)
        right = jnp.where(group == (i - 1) % (lanes // RIM), moved, right)
    pack_l[...] = left
    pack_r[...] = right

    pl.semaphore_wait(barrier, count)

    def copies(dx, dy, n):
        target = {"gx": gx + dx, "gy": gy + dy}

        def remote(src, dst, m):
            return pltpu.make_async_remote_copy(
                src_ref=src, dst_ref=dst, send_sem=send_sem.at[m], recv_sem=recv_sem.at[m],
                device_id=target, device_id_type=MESH,
            )

        if dy == 0:
            first = rows if dx > 0 else RIM
            landing = 0 if dx > 0 else RIM + rows
            return [
                remote(floats.at[:, pl.ds(first, RIM)], floats.at[:, pl.ds(landing, RIM)], n),
                remote(ints.at[:, pl.ds(first, RIM)], ints.at[:, pl.ds(landing, RIM)], 8 + (dx > 0)),
            ]
        src, dst = (pack_r, rim_l) if dy > 0 else (pack_l, rim_r)
        if dx == 0:
            return [remote(src, dst.at[pl.ds(RIM, rows)], n)]
        first = rows - RIM if dx > 0 else 0
        landing = 0 if dx > 0 else RIM + rows
        return [remote(src.at[pl.ds(first, RIM)], dst.at[pl.ds(landing, RIM)], n)]

    order = sorted(range(8), key=lambda n: abs(DIRECTIONS[n][1]))
    for n in order:
        dx, dy = DIRECTIONS[n]

        @pl.when(exists(dx, dy))
        def _(dx=dx, dy=dy, n=n):
            for c in copies(dx, dy, n):
                c.start()

    def arrive(n):
        dx, dy = DIRECTIONS[n]

        @pl.when(exists(-dx, -dy))
        def _():
            for c in copies(dx, dy, n):
                c.wait_recv()

    w = basal_response()
    ext = rows + 2 * RIM
    tall = rows + RIM
    tiles = tall // 8
    wide = 2 * RIM
    slot = lax.broadcasted_iota(jnp.int32, (8, lanes), 1) // wide
    lane_low = jnp.where(gy < ny - 1, lanes + RIM, lanes)
    lane_high = jnp.where(gy > 0, 2 * lanes - RIM, 2 * lanes)

    def in_map_lanes(height):
        lane_i = lax.broadcasted_iota(jnp.int32, (height, 2 * lanes), 1)
        return jnp.logical_or(lane_i < lane_low, lane_i >= lane_high)

    def field_reader(top, height, valid):
        at = slice(top, top + height)
        packed_l, packed_r = rim_l[at], rim_r[at]
        group = lax.broadcasted_iota(jnp.int32, (height, lanes), 1) // RIM

        def field(i, fill):
            main = floats[i, at] if i < 8 else ints[i - 8, at].astype(jnp.float32)
            rim = turn(jnp.where(group == i, packed_r, packed_l), -RIM * i, 1)
            return jnp.where(valid, jnp.concatenate([main, rim], axis=1), fill)

        return field

    def first_velocity(driving, rate, friction, ice):
        viscous = rate * float(FLOOR ** (-1.0 / 3.0))
        speed = driving / (4.0 * viscous)
        drop = -speed * friction / (viscous + friction * float(w[0]))
        return speed * ice, drop * ice

    def squeeze(f, which):
        tile = jnp.zeros((8, lanes), jnp.float32)
        for n, t in enumerate(which):
            moved = turn(f[8 * t : 8 * t + 8, lanes:], wide * n + RIM, 1)
            tile = jnp.where(slot == n, moved, tile)
        return jnp.concatenate([f[8 * t : 8 * t + 8, :lanes] for t in which] + [tile], axis=0)

    def spread(f, count):
        last = f[8 * count :]
        return [
            jnp.concatenate([f[8 * n : 8 * n + 8], turn(last, -(wide * n + RIM), 1)], axis=1)
            for n in range(count)
        ]

    def eliminate(speed, drop, driving, rate, which, offset, lead):
        sxp, sxm, syp, sym = neighbours(speed)
        dxp, dxm, dyp, dym = neighbours(drop)
        sdx, sdy, ddx, ddy = sxp - sxm, syp - sym, dxp - dxm, dyp - dym
        flat = [
            0.03125 * (sdx * sdx + sdy * sdy) + 0.125 * FLOOR,
            0.0625 * (sdx * ddx + sdy * ddy),
            0.03125 * (ddx * ddx + ddy * ddy),
            0.125 * drop * drop,
            0.25 * ((sxp + sxm) + (syp + sym)),
            0.25 * ((dxp + dxm) + (dyp + dym)),
            driving * (0.5 / rate),
        ]
        flat = [squeeze(turn(f, lead, 0), which) for f in flat]
        for n in range(len(which) + 1):
            at = slice(offset + 8 * n, offset + 8 * n + 8)
            c0, c1, c2, c3, n0, n1, dr = [f[8 * n : 8 * n + 8] for f in flat]
            before = None
            for k in range(LAYERS):
                wk = float(w[k])
                strain = c0 + (c1 * wk + c2 * (wk * wk))
                if k < LAYERS - 1:
                    strain = strain + c3 * float((w[k + 1] - w[k]) ** 2)
                twice = jnp.exp2(jnp.log(strain) * THIRD)
                q_ref[k, at] = twice
                r_ref[k, at] = dr + twice * (n0 + n1 * wk)
                if k > 0:
                    g_ref[k - 1, at] = 0.5 * (before + twice)
                before = twice

        at = slice(offset, offset + 8 * (len(which) + 1))
        up_d, up_e, up_t = None, q_ref[0, at], r_ref[0, at]
        down_d, down_e, down_t = None, q_ref[LAYERS - 1, at], r_ref[LAYERS - 1, at]
        product = None

        def step(d, e, t, g, q, r):
            d = e + (g if d is None else g * d)
            return d, q * d + g * e, r * d + g * t

        for k in range(LAYERS - 1):
            j = LAYERS - 2 - k
            g = g_ref[k, at]
            product = g if product is None else product * g
            up_d, up_e, up_t = step(up_d, up_e, up_t, g, q_ref[k + 1, at], r_ref[k + 1, at])
            down_d, down_e, down_t = step(
                down_d, down_e, down_t, g_ref[j, at], q_ref[j, at], r_ref[j, at]
            )
            if k % RESCALE == RESCALE - 1 and k < LAYERS - 2:
                shrink = 1.0 / up_d
                up_d, up_e, up_t, product = None, up_e * shrink, up_t * shrink, product * shrink
                shrink = 1.0 / down_d
                down_d, down_e, down_t = None, down_e * shrink, down_t * shrink
        shrink = 1.0 / up_e
        return down_d, down_e, down_t, up_t * shrink, product * shrink

    def finish(parts, friction, rate, ice, which):
        down_d, down_e, down_t, top, reach = parts
        base = squeeze(turn(friction * (0.5 / rate), -HALF, 0), which)
        mask = squeeze(turn(ice, -HALF, 0), which)
        basal = down_t / (down_e + base * down_d)
        surface = top - base * basal * reach
        return [spread(f * mask, len(which)) for f in (basal, surface)]

    for n in order:
        if DIRECTIONS[n][0] == 0:
            arrive(n)
    early = list(range(1, tiles - 1))
    late = [0, tiles - 1]
    field = field_reader(RIM, rows, in_map_lanes(rows))
    driving, rate = field(0, 0.0), field(1, 1.0)
    speed, drop = first_velocity(driving, rate, field(2, 0.0) * field(9, 0.0), field(8, 0.0))
    early_parts = eliminate(speed, drop, driving, rate, early, 0, HALF)
    for n in order:
        if DIRECTIONS[n][0] != 0:
            arrive(n)

    row_i = lax.broadcasted_iota(jnp.int32, (ext, 2 * lanes), 0)
    row_low = jnp.where(gx > 0, 0, RIM)
    row_high = jnp.where(gx < nx - 1, ext, RIM + rows)
    valid = jnp.logical_and(
        jnp.logical_and(row_i >= row_low, row_i < row_high), in_map_lanes(ext)
    )
    field = field_reader(0, ext, valid)
    driving = field(0, 0.0)
    rate = field(1, 1.0)
    friction = field(2, 0.0)
    melt = field(3, 0.0)
    trans = field(4, 0.0)
    leakage = field(5, 1.0)
    pressure = field(6, 0.0)
    scale = field(7, 0.0)
    ice = field(8, 0.0)
    grounded = field(9, 0.0)
    friction = friction * grounded
    scale = scale * grounded

    speed, drop = first_velocity(driving, rate, friction, ice)
    sliding = speed + drop * float(w[0])
    squared = sliding * sliding
    trans_eff = trans * (1.0 + squared / (1.0 + squared))
    source = melt + HEATING * friction * squared
    pressure = water_solve(pressure, trans_eff, leakage, source, valid)
    friction = scale * pressure

    late_parts = eliminate(speed, drop, driving, rate, late, 8 * (len(early) + 1), -HALF)
    pieces = [None] * tiles
    for parts, which in ((early_parts, early), (late_parts, late)):
        for n, piece in enumerate(zip(*finish(parts, friction, rate, ice, which))):
            pieces[which[n]] = piece
    blank = jnp.zeros((RIM, 2 * lanes), jnp.float32)
    basal = turn(jnp.concatenate([p[0] for p in pieces] + [blank], axis=0), HALF, 0)
    surface = jnp.concatenate([p[1][:, :lanes] for p in pieces], axis=0)
    sliding = jnp.where(valid, basal, 0.0)
    squared = sliding * sliding
    trans_eff = trans * (1.0 + squared / (1.0 + squared))
    source = melt + HEATING * friction * squared
    pressure = water_solve(pressure, trans_eff, leakage, source, valid)
    block = pressure[RIM : RIM + rows, :lanes]
    send_p[...] = block

    def last():
        return pltpu.make_async_remote_copy(
            src_ref=send_p, dst_ref=out.at[0, strip], send_sem=last_send, recv_sem=last_recv.at[strip],
            device_id={"sec": sectors}, device_id_type=MESH,
        )

    @pl.when(sends_last)
    def _():
        last().start()

    @pl.when(is_ice)
    def _():
        out[0, 0] = turn(surface, -HALF, 0)[:rows]
        out[0, 1] = sliding[RIM : RIM + rows, :lanes]
        out[0, 2] = scale[RIM : RIM + rows, :lanes] * block

    @pl.when(jnp.logical_not(is_ice))
    def _():
        out[0, 0] = block

    for n in order:
        dx, dy = DIRECTIONS[n]

        @pl.when(exists(dx, dy))
        def _(dx=dx, dy=dy, n=n):
            for c in copies(dx, dy, n):
                c.wait_send()

    @pl.when(sends_last)
    def _():
        last().wait_send()

    for s in range(1, sectors):

        @pl.when(jnp.logical_not(is_ice))
        def _(s=s):
            pltpu.make_async_remote_copy(
                src_ref=send_p, dst_ref=out.at[0, s], send_sem=last_send, recv_sem=last_recv.at[s],
                device_id={"sec": 0}, device_id_type=MESH,
            ).wait_recv()


def on_device(nx, ny, *args):
    sectors, rows, lanes = args[0].shape
    ext = rows + 2 * RIM
    f32 = jnp.float32
    vmem = pltpu.VMEM
    dma = pltpu.SemaphoreType.DMA
    return pl.pallas_call(
        functools.partial(kernel, sectors, nx, ny),
        out_shape=pltpu.VMEM((1, sectors, rows, lanes), f32),
        in_specs=[pl.BlockSpec(memory_space=pltpu.HBM)] * len(args),
        out_specs=pl.BlockSpec(memory_space=pltpu.VMEM),
        scratch_shapes=[
            vmem((8, ext, lanes), f32),
            vmem((2, ext, lanes), jnp.int32),
            vmem((rows, lanes), f32),
            vmem((rows, lanes), f32),
            vmem((ext, lanes), f32),
            vmem((ext, lanes), f32),
            vmem((LAYERS, ext + RIM, lanes), f32),
            vmem((LAYERS, ext + RIM, lanes), f32),
            vmem((LAYERS, ext + RIM, lanes), f32),
            vmem((rows, lanes), f32),
            dma((2,)),
            dma((10,)),
            dma((10,)),
            dma,
            dma((sectors,)),
        ],
        compiler_params=pltpu.CompilerParams(collective_id=0, has_side_effects=True),
    )(*args)


def solution(mesh):
    spec = P(None, "gx", "gy")
    return jax.shard_map(
        functools.partial(on_device, mesh.shape["gx"], mesh.shape["gy"]),
        mesh=mesh,
        in_specs=(spec,) * 10,
        out_specs=P("sec", None, "gx", "gy"),
        check_vma=False,
    )
```
